32 devices in a mesh: hist: 4 (over y, x), tcol: 8 (over z, core).
Axes of the slice: x: 2, y: 2, z: 4, core: 2. Of those that a mesh axis runs over, the one named last changes fastest.
Arguments:
- history: float32 [8192, 4096], P('hist', 'tcol'), may hold values from -5 to 5
- memory_weight_first: float32 [512, 8192], P(None, 'hist'), may hold values from -0.09375 to 0.09375
- memory_weight_second: float32 [512, 8192], P(None, 'hist'), may hold values from -0.09375 to 0.09375
- link: float32 [512, 512], replicated, may hold values from -0.25 to 0.25
- propagator: float32 [4096, 4096], P(None, 'tcol'), may hold values from -0.09375 to 0.09375
- inverse_one: float32 [512, 512], replicated, as said below
- inverse_two: float32 [512, 512], replicated, as said below
- explicit_first: float32 [512, 4096], P(None, 'tcol'), may hold values from -5 to 5
- explicit_second: float32 [512, 4096], P(None, 'tcol'), may hold values from -5 to 5
Outputs:
- first_slab_rows: float32 [512, 4096], P('hist', 'tcol')
- slab_two: float32 [512, 4096], P('hist', 'tcol')
The draws below stay inside these ranges and needn't reach their ends.
Inputs may be any that keep to these rules, and one draw needn't show every extreme that they name: `inverse_one`: the identity plus independent entries of deviation 0.5 / sqrt(512). `inverse_two`: the identity plus independent entries of deviation 0.5 / sqrt(512).
All inputs are finite; a program needn't handle non-finite values.
Results may differ from the reference program's by a relative error of at most 0.0003.
Values sent between devices are 32-bit elements; how exact they have to be, the bound alone decides.
A program may use at most 128 MiB of HBM per device.

```python
import jax
import jax.numpy as jnp
from jax import lax

S = 512
HT = 8192
NC = 4096


def inverse_common(key, salt):
    sub = jax.random.fold_in(key, salt)
    noise = jax.random.normal(sub, (S, S), jnp.float32)
    return jnp.eye(S, dtype=jnp.float32) + noise * (0.5 / jnp.sqrt(jnp.float32(S)))


def draw_inverse_one(key, part):
    return inverse_common(key, 101)


def draw_inverse_two(key, part):
    return inverse_common(key, 202)


def strengthened(values, stream_key, source, target, parts, factor):
    owner, partner = [(jnp.arange(values.shape[position]) // (values.shape[position] // parts)).reshape([-1 if axis == position else 1 for axis in range(values.ndim)]) for position in (source, target)]
    chosen = jax.random.permutation(stream_key, parts)[partner]
    strong = (owner == chosen) | (owner == (partner + parts // 2) % parts)
    return jnp.where(strong, factor * values, values)


def levels(own_key, extent, split, low, high):
    def one(position, shards_of):
        draws = jax.random.uniform(jax.random.fold_in(jax.random.fold_in(own_key, 6), position), (shards_of,), jnp.float32, low / len(split), high / len(split))
        return jnp.repeat(jnp.exp(draws), extent[position] // shards_of).reshape((-1,) + (1,) * (len(extent) - position - 1))

    loudness = one(*split[0])
    for cut in split[1:]:
        loudness = loudness * one(*cut)
    return loudness


def gaussian(rng, shape, deviation, limit, pieces=(), held_as=jnp.bfloat16):
    level = levels(rng, shape, pieces, -0.22, 0.18) if pieces else 1.0
    drawn = jax.random.normal(rng, shape, jnp.float32) * deviation * level
    return jnp.minimum(jnp.maximum(drawn, -limit), limit).astype(held_as)


def heavy_noise(key, shape, spread, reach, cuts, heavy, kind=jnp.bfloat16):
    result = spread * jax.random.normal(key, shape, jnp.float32)
    if cuts:
        result = result * levels(key, shape, cuts, -0.22, 0.18)
    return jnp.clip(strengthened(result, jax.random.fold_in(key, 3), *heavy), -reach, reach).astype(kind)


def setup_inputs(seed: int = 0) -> dict:
    key_list = jax.random.split(jax.random.key(seed), 10)
    return {
        "history": gaussian(key_list[0], (HT, NC), 0.8, 5.0, ((0, 4), (1, 8)), jnp.float32),
        "memory_weight_first": heavy_noise(key_list[1], (S, HT), HT ** -0.5, 0.09375, ((1, 4),), (1, 0, 4, 2.0), jnp.float32),
        "memory_weight_second": heavy_noise(key_list[2], (S, HT), HT ** -0.5, 0.09375, ((1, 4),), (1, 0, 4, 2.0), jnp.float32),
        "link": gaussian(key_list[3], (S, S), S ** -0.5, 0.25, (), jnp.float32),
        "propagator": gaussian(key_list[4], (NC, NC), NC ** -0.5, 0.09375, ((1, 8),), jnp.float32),
        "inverse_one": draw_inverse_one(jax.random.fold_in(key_list[9], 71), 0),
        "inverse_two": draw_inverse_two(jax.random.fold_in(key_list[9], 71), 0),
        "explicit_first": gaussian(key_list[7], (S, NC), 0.7, 5.0, ((1, 8),), jnp.float32),
        "explicit_second": gaussian(key_list[8], (S, NC), 0.7, 5.0, ((1, 8),), jnp.float32),
    }


strength = 0.2
step_size = 0.5
highest = lax.Precision.HIGHEST


def cubic_power(value):
    return strength * value * value * value


def matrix_product(left, right):
    return jnp.dot(left, right, preferred_element_type=jnp.float32, precision=highest)


def reference(history, memory_weight_first, memory_weight_second, link, propagator, inverse_one, inverse_two, explicit_first, explicit_second):
    self_energy_history = cubic_power(history)
    predictor_first = explicit_first + matrix_product(memory_weight_first, self_energy_history)
    mem_one = matrix_product(cubic_power(predictor_first), propagator)
    first_slab_rows = matrix_product(inverse_one, predictor_first + step_size * mem_one)
    collision_second = matrix_product(memory_weight_second, self_energy_history) + matrix_product(link, cubic_power(first_slab_rows))
    predictor_second = explicit_second + collision_second
    mem_two = matrix_product(cubic_power(predictor_second), propagator)
    slab_two = matrix_product(inverse_two, predictor_second + step_size * mem_two)
    return first_slab_rows, slab_two
```

```python
import functools

import jax
import jax.numpy as jnp
from jax import lax
from jax.experimental import pallas as pl
from jax.experimental.pallas import tpu as pltpu
from jax.sharding import PartitionSpec as P

strength = 0.2
step_size = 0.5
MESH = pl.DeviceIdType.MESH
f32 = jnp.float32
bf16 = jnp.bfloat16


def cubic_power(value):
    return strength * value * value * value


def halves(value):
    high = value.astype(bf16)
    return high, (value - high.astype(f32)).astype(bf16)


def mm(left, right):
    return jnp.dot(left, right, preferred_element_type=f32)


def product(left, right_high, right_low):
    m = left.shape[0]
    high, low = halves(left)
    both = mm(jnp.concatenate([high, low], axis=0), right_high)
    return both[:m] + both[m:] + mm(high, right_low)


def kernel(
    H, T, C,
    hist_ref, w1_ref, w2_ref, link_ref, prop_ref, inv1_ref, inv2_ref, e1_ref, e2_ref,
    o1_ref, o2_ref,
    hbuf, wbuf, wh, wl, sh, sl, ph, plo, mat, ih, il, kh, kl, inv2, e1, e2,
    part, rs, pred, acc1, g1, g2, rf, nf, xh, xl, s1, p2h, p2l, qh, ql, base,
    hsem, wsem, psem, msem, rs_send, rs_recv, rf_send, rf_recv, nf_send, nf_recv,
    sp, sr, sleft, rz, rp,
):
    K, N = hist_ref.shape
    S = w1_ref.shape[0]
    R = S // H
    Rc = R // C
    Nc = N // C
    nK = K // N
    Z = T // 2
    h = lax.axis_index("hist")
    t = lax.axis_index("tcol")
    p = t // 2
    core = t % 2
    other = 1 - core
    tile = 32

    def split(source, high, low, rows, function=lambda v: v):
        @pl.loop(0, rows // tile)
        def _(i):
            at = pl.ds(pl.multiple_of(i * tile, tile), tile)
            a, b = halves(function(source[at, :]))
            high[at, :] = a
            low[at, :] = b

    def hist_copy(kb):
        return pltpu.make_async_copy(hist_ref.at[pl.ds(kb * N, N), :], hbuf.at[kb], hsem.at[kb])

    def w_copy(w, c, j):
        ref = (w1_ref, w2_ref)[w]
        return pltpu.make_async_copy(
            ref.at[pl.ds(j * R + c * Rc, Rc), :], wbuf.at[w, c, j], wsem.at[w, c, j]
        )

    def p_copy(b):
        return pltpu.make_async_copy(
            prop_ref.at[pl.ds(b * N, N), :], hbuf.at[b % nK], psem.at[b]
        )

    own_rows = pl.ds(pl.multiple_of(h * R, R), R)
    small = (
        pltpu.make_async_copy(e1_ref.at[own_rows, :], e1, msem.at[0]),
        pltpu.make_async_copy(inv1_ref, mat.at[0], msem.at[1]),
        pltpu.make_async_copy(link_ref, mat.at[1], msem.at[2]),
        pltpu.make_async_copy(inv2_ref.at[own_rows, :], inv2, msem.at[3]),
        pltpu.make_async_copy(e2_ref, e2, msem.at[4]),
    )

    for kb in range(nK):
        hist_copy(kb).start()
    for c in range(C):
        for j in range(H):
            w_copy(0, c, j).start()
    small[0].start()

    barrier = pltpu.get_barrier_semaphore()

    def greet(device):
        pl.semaphore_signal(barrier, inc=1, device_id=device, device_id_type=MESH)

    for d in range(1, H):
        greet({"hist": lax.rem(h + d, H)})
    greet({"tcol": p * 2 + other})

    greet({"tcol": lax.rem(p + 1, Z) * 2 + core})
    greet({"tcol": lax.rem(p + Z - 1, Z) * 2 + core})

    for kb in range(nK):
        hist_copy(kb).wait()
        split(hbuf.at[kb], sh.at[kb], sl.at[kb], N, cubic_power)

    for c in range(C):
        for j in range(H):
            w_copy(1, c, j).start()
    for copy in small[1:]:
        copy.start()
    for b in range(nK):
        p_copy(b).start()

    def history_sum(w, c):
        for j in range(H):
            w_copy(w, c, j).wait()
            split(wbuf.at[w, c, j], wh.at[j], wl.at[j], Rc)

        for kb in range(nK):
            cols = pl.ds(kb * N, N)
            a = wh[:, :, cols].reshape(H * Rc, N)
            b = wl[:, :, cols].reshape(H * Rc, N)
            value = mm(a, sh[kb]) + mm(b, sh[kb]) + mm(a, sl[kb])
            value = value.reshape(H, Rc, N)
            if kb == 0:
                part[w, c] = value
            else:
                part[w, c] += value

    def rs_copy(w, c, d):
        dst = lax.rem(h + d, H)
        return pltpu.make_async_remote_copy(
            src_ref=part.at[w, c, dst], dst_ref=rs.at[w, c, d - 1],
            send_sem=rs_send.at[w, c, d - 1], recv_sem=rs_recv.at[w, c, d - 1],
            device_id={"hist": dst}, device_id_type=MESH,
        )

    def gathered(w, c):
        total = part[w, c, h]
        for d in range(1, H):
            rs_copy(w, c, d).wait_recv()
            total += rs[w, c, d - 1]
        return total

    def z_copy(g, st, c, q, where):
        block = g.at[c, 2 * q + core]
        send, recv, target = {
            "partner": (sp, rp, p * 2 + other),
            "right": (sr, rz, t + 2),
            "left": (sleft, rz, t - 2),
        }[where]
        return pltpu.make_async_remote_copy(
            src_ref=block, dst_ref=block,
            send_sem=send.at[st, c, q], recv_sem=recv.at[st, c, q],
            device_id={"tcol": target}, device_id_type=MESH,
        )

    def z_partner_wait(g, st, c, q):
        block = g.at[c, 2 * q + other]
        pltpu.make_async_remote_copy(
            src_ref=block, dst_ref=block,
            send_sem=sp.at[st, c, q], recv_sem=rp.at[st, c, q],
            device_id={"tcol": p * 2 + other}, device_id_type=MESH,
        ).wait_recv()

    def z_own(g, st, c):
        @pl.when(p + 1 < Z)
        def _():
            z_copy(g, st, c, p, "right").start()

        @pl.when(p > 0)
        def _():
            z_copy(g, st, c, p, "left").start()

        z_copy(g, st, c, p, "partner").start()

    def z_step(g, st, c, s, use):
        @pl.when(p >= s)
        def _():
            q = p - s
            z_copy(g, st, c, q, "right").wait_recv()

            @pl.when(p + 1 < Z)
            def _():
                z_copy(g, st, c, q, "right").start()

            z_copy(g, st, c, q, "partner").start()

        @pl.when(p + s < Z)
        def _():
            q = p + s
            z_copy(g, st, c, q, "left").wait_recv()

            @pl.when(p > 0)
            def _():
                z_copy(g, st, c, q, "left").start()

            z_copy(g, st, c, q, "partner").start()

        @pl.when(p >= s)
        def _():
            use(c, 2 * (p - s) + core)

        @pl.when(p + s < Z)
        def _():
            use(c, 2 * (p + s) + core)

        @pl.when(p >= s)
        def _():
            z_partner_wait(g, st, c, p - s)
            use(c, 2 * (p - s) + other)

        @pl.when(p + s < Z)
        def _():
            z_partner_wait(g, st, c, p + s)
            use(c, 2 * (p + s) + other)

    def z_finish(g, st, c):
        z_copy(g, st, c, p, "partner").wait_send()

        @pl.when(p + 1 < Z)
        def _():
            z_copy(g, st, c, p, "right").wait_send()

        @pl.when(p > 0)
        def _():
            z_copy(g, st, c, p, "left").wait_send()

        for s in range(1, Z):
            @pl.when(p >= s)
            def _():
                z_copy(g, st, c, p - s, "partner").wait_send()

                @pl.when(p + 1 < Z)
                def _():
                    z_copy(g, st, c, p - s, "right").wait_send()

            @pl.when(p + s < Z)
            def _():
                z_copy(g, st, c, p + s, "partner").wait_send()

                @pl.when(p > 0)
                def _():
                    z_copy(g, st, c, p + s, "left").wait_send()

    def use_one(c, b):
        acc1[c] += product(g1[c, b], ph[b], plo[b])

    def use_two(c, b):
        rows = pl.ds(c * Nc, Nc)
        base[...] += product(g2[c, b], ph[b, rows, :], plo[b, rows, :])

    history_sum(0, 0)
    pl.semaphore_wait(barrier, H + 2)

    for d in range(1, H):
        rs_copy(0, 0, d).start()
    for c in range(1, C):
        history_sum(0, c)
        for d in range(1, H):
            rs_copy(0, c, d).start()

    small[0].wait()

    def begin_one(c):
        value = gathered(0, c) + e1[pl.ds(c * Rc, Rc), :]
        pred[c] = value
        g1[c, t] = cubic_power(value)
        z_own(g1, 0, c)

    for c in range(C):
        history_sum(1, c)
        for d in range(1, H):
            rs_copy(1, c, d).start()
        if c == 0:
            begin_one(0)

    for b in range(T):
        p_copy(b).wait()
        split(hbuf.at[b % nK], ph.at[b], plo.at[b], N)
        if b + nK < T:
            p_copy(b + nK).start()

    def local_one(c):
        acc1[c] = product(g1[c, t], ph[t], plo[t])
        z_partner_wait(g1, 0, c, p)
        use_one(c, 2 * p + other)

    local_one(0)
    for c in range(1, C):
        if c == 1:
            z_step(g1, 0, 0, 1, use_one)
        begin_one(c)
        local_one(c)
        z_step(g1, 0, c, 1, use_one)

    for copy in small[1:]:
        copy.wait()
    split(mat.at[0], ih, il, S)
    split(mat.at[1], kh, kl, S)

    def nf_copy(d):
        dst = lax.rem(h + d, H)
        return pltpu.make_async_remote_copy(
            src_ref=nf.at[h], dst_ref=nf.at[h],
            send_sem=nf_send.at[d - 1], recv_sem=nf_recv.at[d - 1],
            device_id={"hist": dst}, device_id_type=MESH,
        )

    def nf_wait(d):
        src = lax.rem(h + H - d, H)
        pltpu.make_async_remote_copy(
            src_ref=nf.at[src], dst_ref=nf.at[src],
            send_sem=nf_send.at[d - 1], recv_sem=nf_recv.at[d - 1],
            device_id={"hist": src}, device_id_type=MESH,
        ).wait_recv()

    for s in range(2, Z):
        for c in range(C):
            z_step(g1, 0, c, s, use_one)
        if s == max(2, Z // 2):
            for c in range(C):
                nf[h, pl.ds(c * Rc, Rc), :] = gathered(1, c)
            for d in range(1, H):
                nf_copy(d).start()

    def rf_copy(c, d):
        dst = lax.rem(h + d, H)
        return pltpu.make_async_remote_copy(
            src_ref=rf.at[c, h], dst_ref=rf.at[c, h],
            send_sem=rf_send.at[c, d - 1], recv_sem=rf_recv.at[c, d - 1],
            device_id={"hist": dst}, device_id_type=MESH,
        )

    def rf_wait(c, d):
        src = lax.rem(h + H - d, H)
        pltpu.make_async_remote_copy(
            src_ref=rf.at[c, src], dst_ref=rf.at[c, src],
            send_sem=rf_send.at[c, d - 1], recv_sem=rf_recv.at[c, d - 1],
            device_id={"hist": src}, device_id_type=MESH,
        ).wait_recv()

    for cc in range(C):
        cols = pl.ds(cc * Nc, Nc)
        for c in range(C):
            rf[cc, h, pl.ds(c * Rc, Rc), :] = pred[c, :, cols] + step_size * acc1[c, :, cols]
        for d in range(1, H):
            rf_copy(cc, d).start()

    base[...] = jnp.zeros_like(base)

    def second(cc):
        cols = pl.ds(cc * Nc, Nc)
        for d in range(1, H):
            rf_wait(cc, d)

        @pl.loop(0, H)
        def _(j):
            split(rf.at[cc, j], xh.at[j], xl.at[j], R)

        a, b = xh[...].reshape(S, Nc), xl[...].reshape(S, Nc)

        @pl.loop(0, H)
        def _(j):
            rows = pl.ds(pl.multiple_of(j * R, R), R)
            left, low = ih[rows, :], il[rows, :]
            s1[rows, :] = mm(left, a) + mm(low, a) + mm(left, b)

        o1_ref[:, cols] = s1[own_rows, :]
        split(s1, p2h, p2l, S, cubic_power)
        if cc == 0:
            for d in range(1, H):
                nf_wait(d)
        a, b = p2h[...], p2l[...]

        @pl.loop(0, H)
        def _(j):
            rows = pl.ds(pl.multiple_of(j * R, R), R)
            left, low = kh[rows, :], kl[rows, :]
            value = mm(left, a) + mm(low, a) + mm(left, b)
            s1[rows, :] = value + nf[j, :, cols] + e2[rows, cols]

        split(s1, p2h, p2l, S)
        split(s1, qh, ql, S, lambda v: step_size * cubic_power(v))
        g2[cc, t] = product(inv2[...], qh[...], ql[...])
        z_own(g2, 1, cc)
        base[:, cols] += product(inv2[...], p2h[...], p2l[...])
        use_two(cc, t)
        z_partner_wait(g2, 1, cc, p)
        use_two(cc, 2 * p + other)

    for cc in range(C):
        second(cc)
        z_step(g2, 1, cc, 1, use_two)
    for s in range(2, Z):
        for cc in range(C):
            z_step(g2, 1, cc, s, use_two)
    o2_ref[...] = base[...]

    for c in range(C):
        for d in range(1, H):
            rs_copy(0, c, d).wait_send()
            rs_copy(1, c, d).wait_send()
            rf_copy(c, d).wait_send()
        z_finish(g1, 0, c)
        z_finish(g2, 1, c)
    for d in range(1, H):
        nf_copy(d).wait_send()


def shards(*operands):
    history, w1 = operands[:2]
    K, N = history.shape
    S = w1.shape[0]
    H, T, C = lax.axis_size("hist"), lax.axis_size("tcol"), 2
    R = S // H
    Rc, Nc, nK, Z = R // C, N // C, K // N, T // 2
    V, D = pltpu.VMEM, pltpu.SemaphoreType.DMA
    return pl.pallas_call(
        functools.partial(kernel, H, T, C),
        out_shape=[jax.ShapeDtypeStruct((R, N), f32)] * 2,
        in_specs=[pl.BlockSpec(memory_space=pl.ANY)] * 9,
        out_specs=[pl.BlockSpec(memory_space=pltpu.VMEM)] * 2,
        scratch_shapes=[
            V((nK, N, N), f32), V((2, C, H, Rc, K), f32),
            V((H, Rc, K), bf16), V((H, Rc, K), bf16),
            V((nK, N, N), bf16), V((nK, N, N), bf16),
            V((T, N, N), bf16), V((T, N, N), bf16),
            V((2, S, S), f32),
            V((S, S), bf16), V((S, S), bf16), V((S, S), bf16), V((S, S), bf16),
            V((R, S), f32), V((R, N), f32), V((S, N), f32),
            V((2, C, H, Rc, N), f32), V((2, C, H - 1, Rc, N), f32),
            V((C, Rc, N), f32), V((C, Rc, N), f32),
            V((C, T, Rc, N), f32), V((C, T, R, Nc), f32),
            V((C, H, R, Nc), f32), V((H, R, N), f32),
            V((H, R, Nc), bf16), V((H, R, Nc), bf16),
            V((S, Nc), f32),
            V((S, Nc), bf16), V((S, Nc), bf16), V((S, Nc), bf16), V((S, Nc), bf16),
            V((R, N), f32),
            D((nK,)), D((2, C, H)), D((T,)), D((5,)),
            D((2, C, H - 1)), D((2, C, H - 1)),
            D((C, H - 1)), D((C, H - 1)), D((H - 1,)), D((H - 1,)),
            D((2, C, Z)), D((2, C, Z)), D((2, C, Z)), D((2, C, Z)), D((2, C, Z)),
        ],
        compiler_params=pltpu.CompilerParams(
            collective_id=0, has_side_effects=True, vmem_limit_bytes=64 * 1024 * 1024 - 65536
        ),
    )(*operands)


def solution(mesh):
    return jax.shard_map(
        shards,
        mesh=mesh,
        in_specs=(
            P("hist", "tcol"),
            P(None, "hist"),
            P(None, "hist"),
            P(),
            P(None, "tcol"),
            P(),
            P(),
            P(None, "tcol"),
            P(None, "tcol"),
        ),
        out_specs=(P("hist", "tcol"), P("hist", "tcol")),
        check_vma=False,
    )
```

```python
import functools

import jax
import jax.numpy as jnp
from jax import lax
from jax.experimental import pallas as pl
from jax.experimental.pallas import tpu as pltpu
from jax.sharding import PartitionSpec as P

strength = 0.2
step_size = 0.5
MESH = pl.DeviceIdType.MESH
f32 = jnp.float32
bf16 = jnp.bfloat16


def cubic_power(value):
    return strength * value * value * value


def halves(value):
    high = value.astype(bf16)
    return high, (value - high.astype(f32)).astype(bf16)


def mm(left, right):
    return jnp.dot(left, right, preferred_element_type=f32)


def product(left, right_high, right_low):
    m = left.shape[0]
    high, low = halves(left)
    both = mm(jnp.concatenate([high, low], axis=0), right_high)
    return both[:m] + both[m:] + mm(high, right_low)


def kernel(
    H, T, C,
    hist_ref, w1_ref, w2_ref, link_ref, prop_ref, inv1_ref, inv2_ref, e1_ref, e2_ref,
    o1_ref, o2_ref,
    hbuf, wbuf, wh, wl, sh, sl, ph, plo, mat, ih, il, kh, kl, vh, vl, e1, e2,
    part, rs, pred, acc1, acc2, g1, g2, nsend, nrecv, near, rsend, rf, s1, s2, orecv,
    ysend, yrecv, bsend, brecv, xh, xl, p2h, p2l, qh, ql,
    hsem, wsem, psem, msem, rs_send, rs_recv, x_sent, x_got,
    sp, sr, sleft, rz, rp,
):
    K, N = hist_ref.shape
    S = w1_ref.shape[0]
    R = S // H
    Rc = R // C
    Nh = N // H
    nK = K // N
    Z = T // 2
    h = lax.axis_index("hist")
    t = lax.axis_index("tcol")
    p = t // 2
    core = t % 2
    other = 1 - core
    tile = 32

    def split(source, high, low, rows, function=lambda v: v):
        @pl.loop(0, rows // tile)
        def _(i):
            at = pl.ds(pl.multiple_of(i * tile, tile), tile)
            a, b = halves(function(source[at, :]))
            high[at, :] = a
            low[at, :] = b

    def hist_copy(kb):
        return pltpu.make_async_copy(hist_ref.at[pl.ds(kb * N, N), :], hbuf.at[kb], hsem.at[kb])

    def w_copy(w, c, j):
        ref = (w1_ref, w2_ref)[w]
        return pltpu.make_async_copy(
            ref.at[pl.ds(j * R + c * Rc, Rc), :], wbuf.at[w, c, j], wsem.at[w, c, j]
        )

    def p_copy(b):
        return pltpu.make_async_copy(
            prop_ref.at[pl.ds(b * N, N), :], hbuf.at[b % nK], psem.at[b]
        )

    own_rows = pl.ds(pl.multiple_of(h * R, R), R)
    small = (
        pltpu.make_async_copy(e1_ref.at[own_rows, :], e1, msem.at[0]),
        pltpu.make_async_copy(inv1_ref, mat.at[0], msem.at[1]),
        pltpu.make_async_copy(link_ref, mat.at[1], msem.at[2]),
        pltpu.make_async_copy(inv2_ref, mat.at[2], msem.at[3]),
        pltpu.make_async_copy(e2_ref.at[own_rows, :], e2, msem.at[4]),
    )

    for kb in range(nK):
        hist_copy(kb).start()
    for c in range(C):
        for j in range(H):
            w_copy(0, c, j).start()
    small[0].start()

    barrier = pltpu.get_barrier_semaphore()

    def greet(device):
        pl.semaphore_signal(barrier, inc=1, device_id=device, device_id_type=MESH)

    for d in range(1, H):
        greet({"hist": lax.rem(h + d, H)})
    greet({"tcol": p * 2 + other})

    greet({"tcol": lax.rem(p + 1, Z) * 2 + core})
    greet({"tcol": lax.rem(p + Z - 1, Z) * 2 + core})

    for kb in range(nK):
        hist_copy(kb).wait()
        split(hbuf.at[kb], sh.at[kb], sl.at[kb], N, cubic_power)

    for c in range(C):
        for j in range(H):
            w_copy(1, c, j).start()
    for copy in small[1:]:
        copy.start()
    for b in range(nK):
        p_copy(b).start()

    def history_sum(w, c):
        for j in range(H):
            w_copy(w, c, j).wait()
            split(wbuf.at[w, c, j], wh.at[j], wl.at[j], Rc)

        for kb in range(nK):
            cols = pl.ds(kb * N, N)
            a = wh[:, :, cols].reshape(H * Rc, N)
            b = wl[:, :, cols].reshape(H * Rc, N)
            value = mm(a, sh[kb]) + mm(b, sh[kb]) + mm(a, sl[kb])
            value = value.reshape(H, Rc, N)
            if kb == 0:
                part[w, c] = value
            else:
                part[w, c] += value

    def rs_copy(c, d):
        dst = lax.rem(h + d, H)
        return pltpu.make_async_remote_copy(
            src_ref=part.at[0, c, dst], dst_ref=rs.at[c, d - 1],
            send_sem=rs_send.at[c, d - 1], recv_sem=rs_recv.at[c, d - 1],
            device_id={"hist": dst}, device_id_type=MESH,
        )

    def gathered(c):
        total = part[0, c, h]
        for d in range(1, H):
            rs_copy(c, d).wait_recv()
            total += rs[c, d - 1]
        return total

    def exchange(kind, d, source, target):
        dst = lax.rem(h + d, H)
        return pltpu.make_async_remote_copy(
            src_ref=source(dst), dst_ref=target(h, d),
            send_sem=x_sent.at[kind, d - 1], recv_sem=x_got.at[kind, d - 1],
            device_id={"hist": dst}, device_id_type=MESH,
        )

    def arrived(kind, d, target):
        src = lax.rem(h + H - d, H)
        ref = target(src, d)
        pltpu.make_async_remote_copy(
            src_ref=ref, dst_ref=ref,
            send_sem=x_sent.at[kind, d - 1], recv_sem=x_got.at[kind, d - 1],
            device_id={"hist": src}, device_id_type=MESH,
        ).wait_recv()

    plans = {}
    for c in range(C):
        plans[c] = (
            lambda dst, c=c: nsend.at[c, dst], lambda src, d, c=c: nrecv.at[c, d - 1])
        plans[C + c] = (
            lambda dst, c=c: rsend.at[c, dst], lambda src, d, c=c: rf.at[c, src])
        plans[2 * C + c] = (
            lambda dst, c=c: ysend.at[c, dst], lambda src, d, c=c: yrecv.at[c, src])
    plans[3 * C] = (lambda dst: s1.at[dst], lambda src, d: orecv.at[src])
    plans[3 * C + 1] = (lambda dst: bsend.at[dst], lambda src, d: brecv.at[src])

    def x_start(kind):
        for d in range(1, H):
            exchange(kind, d, *plans[kind]).start()

    def x_wait(kind):
        for d in range(1, H):
            arrived(kind, d, plans[kind][1])

    def z_copy(g, st, c, q, where):
        block = g.at[c, 2 * q + core]
        send, recv, target = {
            "partner": (sp, rp, p * 2 + other),
            "right": (sr, rz, t + 2),
            "left": (sleft, rz, t - 2),
        }[where]
        return pltpu.make_async_remote_copy(
            src_ref=block, dst_ref=block,
            send_sem=send.at[st, c, q], recv_sem=recv.at[st, c, q],
            device_id={"tcol": target}, device_id_type=MESH,
        )

    def z_partner_wait(g, st, c, q):
        block = g.at[c, 2 * q + other]
        pltpu.make_async_remote_copy(
            src_ref=block, dst_ref=block,
            send_sem=sp.at[st, c, q], recv_sem=rp.at[st, c, q],
            device_id={"tcol": p * 2 + other}, device_id_type=MESH,
        ).wait_recv()

    def z_own(g, st, c):
        @pl.when(p + 1 < Z)
        def _():
            z_copy(g, st, c, p, "right").start()

        @pl.when(p > 0)
        def _():
            z_copy(g, st, c, p, "left").start()

        z_copy(g, st, c, p, "partner").start()

    def z_step(g, st, c, s, use):
        @pl.when(p >= s)
        def _():
            q = p - s
            z_copy(g, st, c, q, "right").wait_recv()

            @pl.when(p + 1 < Z)
            def _():
                z_copy(g, st, c, q, "right").start()

            z_copy(g, st, c, q, "partner").start()

        @pl.when(p + s < Z)
        def _():
            q = p + s
            z_copy(g, st, c, q, "left").wait_recv()

            @pl.when(p > 0)
            def _():
                z_copy(g, st, c, q, "left").start()

            z_copy(g, st, c, q, "partner").start()

        @pl.when(p >= s)
        def _():
            use(c, 2 * (p - s) + core)

        @pl.when(p + s < Z)
        def _():
            use(c, 2 * (p + s) + core)

        @pl.when(p >= s)
        def _():
            z_partner_wait(g, st, c, p - s)
            use(c, 2 * (p - s) + other)

        @pl.when(p + s < Z)
        def _():
            z_partner_wait(g, st, c, p + s)
            use(c, 2 * (p + s) + other)

    def z_finish(g, st, c):
        z_copy(g, st, c, p, "partner").wait_send()

        @pl.when(p + 1 < Z)
        def _():
            z_copy(g, st, c, p, "right").wait_send()

        @pl.when(p > 0)
        def _():
            z_copy(g, st, c, p, "left").wait_send()

        for s in range(1, Z):
            @pl.when(p >= s)
            def _():
                z_copy(g, st, c, p - s, "partner").wait_send()

                @pl.when(p + 1 < Z)
                def _():
                    z_copy(g, st, c, p - s, "right").wait_send()

            @pl.when(p + s < Z)
            def _():
                z_copy(g, st, c, p + s, "partner").wait_send()

                @pl.when(p > 0)
                def _():
                    z_copy(g, st, c, p + s, "left").wait_send()

    def use_one(c, b):
        acc1[c] += product(g1[c, b], ph[b], plo[b])

    def use_two(c, b):
        acc2[c] += product(g2[c, b], ph[b], plo[b])

    history_sum(0, 0)
    pl.semaphore_wait(barrier, H + 2)

    for d in range(1, H):
        rs_copy(0, d).start()
    for c in range(1, C):
        history_sum(0, c)
        for d in range(1, H):
            rs_copy(c, d).start()

    small[0].wait()

    def begin_one(c):
        value = gathered(c) + e1[pl.ds(c * Rc, Rc), :]
        pred[c] = value
        g1[c, t] = cubic_power(value)
        z_own(g1, 0, c)

    small[4].wait()
    for c in range(C):
        history_sum(1, c)
        part[1, c, h] += e2[pl.ds(c * Rc, Rc), :]
        for j in range(H):
            nsend[c, j] = part[1, c, :, :, j * Nh:(j + 1) * Nh]
        x_start(c)
        if c == 0:
            begin_one(0)

    for b in range(T):
        p_copy(b).wait()
        split(hbuf.at[b % nK], ph.at[b], plo.at[b], N)
        if b + nK < T:
            p_copy(b + nK).start()

    def local_one(c):
        acc1[c] = product(g1[c, t], ph[t], plo[t])
        z_partner_wait(g1, 0, c, p)
        use_one(c, 2 * p + other)

    local_one(0)
    for c in range(1, C):
        if c == 1:
            z_step(g1, 0, 0, 1, use_one)
        begin_one(c)
        local_one(c)
        z_step(g1, 0, c, 1, use_one)

    for copy in small[1:4]:
        copy.wait()
    split(mat.at[0], ih, il, S)
    split(mat.at[1], kh, kl, S)
    split(mat.at[2], vh, vl, S)

    def send_right(c):
        value = pred[c] + step_size * acc1[c]
        for j in range(H):
            rsend[c, j] = value[:, j * Nh:(j + 1) * Nh]
        x_start(C + c)
        rf[c, h] = rsend[c, h]

    def sum_near():
        for c in range(C):
            x_wait(c)
            total = nsend[c, h]
            for d in range(1, H):
                total += nrecv[c, d - 1]
            near[:, c] = total

    for s in range(2, Z):
        for c in range(C):
            z_step(g1, 0, c, s, use_one)
            if s == Z - 1:
                send_right(c)
    if Z == 2:
        for c in range(C):
            send_right(c)
    sum_near()

    for c in range(C):
        x_wait(C + c)

        @pl.loop(0, H)
        def _(j):
            a, b = halves(rf[c, j])
            xh[j, c] = a
            xl[j, c] = b

    def apply(high, low, j, a, b):
        rows = pl.ds(pl.multiple_of(j * R, R), R)
        left, rest = high[rows, :], low[rows, :]
        return mm(left, a) + mm(rest, a) + mm(left, b)

    a, b = xh[...].reshape(S, Nh), xl[...].reshape(S, Nh)

    @pl.loop(0, H)
    def _(j):
        value = apply(ih, il, j, a, b)
        s1[j] = value
        p2h[j], p2l[j] = halves(cubic_power(value))

    a, b = p2h[...].reshape(S, Nh), p2l[...].reshape(S, Nh)

    @pl.loop(0, H)
    def _(j):
        value = apply(kh, kl, j, a, b) + near[j].reshape(R, Nh)
        s2[j] = value
        qh[j], ql[j] = halves(step_size * cubic_power(value))

    a, b = qh[...].reshape(S, Nh), ql[...].reshape(S, Nh)

    @pl.loop(0, H)
    def _(j):
        value = apply(vh, vl, j, a, b)
        for c in range(C):
            ysend[c, j] = value[c * Rc:(c + 1) * Rc, :]

    for c in range(C):
        x_start(2 * C + c)
        yrecv[c, h] = ysend[c, h]
    x_start(3 * C)
    orecv[h] = s1[h]

    @pl.loop(0, H)
    def _(j):
        p2h[j], p2l[j] = halves(s2[j])

    a, b = p2h[...].reshape(S, Nh), p2l[...].reshape(S, Nh)

    @pl.loop(0, H)
    def _(j):
        bsend[j] = apply(vh, vl, j, a, b)

    def begin_two(c):
        x_wait(2 * C + c)
        g2[c, t] = jnp.concatenate([yrecv[c, j] for j in range(H)], axis=1)
        z_own(g2, 1, c)

    def local_two(c):
        acc2[c] = product(g2[c, t], ph[t], plo[t])
        z_partner_wait(g2, 1, c, p)
        use_two(c, 2 * p + other)

    for c in range(C):
        begin_two(c)
    x_start(3 * C + 1)
    brecv[h] = bsend[h]
    for c in range(C):
        local_two(c)
        z_step(g2, 1, c, 1, use_two)
    x_wait(3 * C)
    for j in range(H):
        o1_ref[:, j * Nh:(j + 1) * Nh] = orecv[j]
    for s in range(2, Z):
        for c in range(C):
            z_step(g2, 1, c, s, use_two)
    x_wait(3 * C + 1)
    for c in range(C):
        rows = pl.ds(c * Rc, Rc)
        o2_ref[rows, :] = acc2[c] + jnp.concatenate([brecv[j, rows, :] for j in range(H)], axis=1)

    for c in range(C):
        for d in range(1, H):
            rs_copy(c, d).wait_send()
        z_finish(g1, 0, c)
        z_finish(g2, 1, c)
    for kind in range(3 * C + 2):
        for d in range(1, H):
            exchange(kind, d, *plans[kind]).wait_send()


def shards(*operands):
    history, w1 = operands[:2]
    K, N = history.shape
    S = w1.shape[0]
    H, T, C = lax.axis_size("hist"), lax.axis_size("tcol"), 2
    R = S // H
    Rc, Nh, nK, Z = R // C, N // H, K // N, T // 2
    V, D = pltpu.VMEM, pltpu.SemaphoreType.DMA
    return pl.pallas_call(
        functools.partial(kernel, H, T, C),
        out_shape=[jax.ShapeDtypeStruct((R, N), f32)] * 2,
        in_specs=[pl.BlockSpec(memory_space=pl.ANY)] * 9,
        out_specs=[pl.BlockSpec(memory_space=pltpu.VMEM)] * 2,
        scratch_shapes=[
            V((nK, N, N), f32), V((2, C, H, Rc, K), f32),
            V((H, Rc, K), bf16), V((H, Rc, K), bf16),
            V((nK, N, N), bf16), V((nK, N, N), bf16),
            V((T, N, N), bf16), V((T, N, N), bf16),
            V((3, S, S), f32),
            *[V((S, S), bf16)] * 6,
            V((R, N), f32), V((R, N), f32),
            V((2, C, H, Rc, N), f32), V((C, H - 1, Rc, N), f32),
            V((C, Rc, N), f32), V((C, Rc, N), f32), V((C, Rc, N), f32),
            V((C, T, Rc, N), f32), V((C, T, Rc, N), f32),
            V((C, H, H, Rc, Nh), f32), V((C, H - 1, H, Rc, Nh), f32), V((H, C, Rc, Nh), f32),
            V((C, H, Rc, Nh), f32), V((C, H, Rc, Nh), f32),
            V((H, R, Nh), f32), V((H, R, Nh), f32), V((H, R, Nh), f32),
            V((C, H, Rc, Nh), f32), V((C, H, Rc, Nh), f32),
            V((H, R, Nh), f32), V((H, R, Nh), f32),
            V((H, C, Rc, Nh), bf16), V((H, C, Rc, Nh), bf16),
            *[V((H, R, Nh), bf16)] * 4,
            D((nK,)), D((2, C, H)), D((T,)), D((5,)),
            D((C, H - 1)), D((C, H - 1)), D((3 * C + 2, H - 1)), D((3 * C + 2, H - 1)),
            D((2, C, Z)), D((2, C, Z)), D((2, C, Z)), D((2, C, Z)), D((2, C, Z)),
        ],
        compiler_params=pltpu.CompilerParams(
            collective_id=0, has_side_effects=True, vmem_limit_bytes=64 * 1024 * 1024 - 65536
        ),
    )(*operands)


def solution(mesh):
    return jax.shard_map(
        shards,
        mesh=mesh,
        in_specs=(
            P("hist", "tcol"),
            P(None, "hist"),
            P(None, "hist"),
            P(),
            P(None, "tcol"),
            P(),
            P(),
            P(None, "tcol"),
            P(None, "tcol"),
        ),
        out_specs=(P("hist", "tcol"), P("hist", "tcol")),
        check_vma=False,
    )
```

```python
import functools

import jax
import jax.numpy as jnp
from jax import lax
from jax.experimental import pallas as pl
from jax.experimental.pallas import tpu as pltpu
from jax.sharding import PartitionSpec as P

strength = 0.2
step_size = 0.5
MESH = pl.DeviceIdType.MESH
f32 = jnp.float32
bf16 = jnp.bfloat16


def cubic_power(value):
    return strength * value * value * value


def halves(value):
    high = value.astype(bf16)
    return high, (value - high.astype(f32)).astype(bf16)


def mm(left, right):
    return jnp.dot(left, right, preferred_element_type=f32)


def product(left, right_high, right_low):
    m = left.shape[0]
    high, low = halves(left)
    both = mm(jnp.concatenate([high, low], axis=0), right_high)
    return both[:m] + both[m:] + mm(high, right_low)


def kernel(
    H, T, C,
    hist_ref, w1_ref, w2_ref, link_ref, prop_ref, inv1_ref, inv2_ref, e1_ref, e2_ref,
    o1_ref, o2_ref,
    hbuf, wbuf, wh, wl, sh, sl, ph, plo, mat, ih, il, kh, kl, vh, vl, e1, e2,
    part, rs, pred, acc1, acc2, g1, g2, nsend, nrecv, near, rsend, rf, s1, s2, orecv,
    ysend, yrecv, bsend, brecv, xh, xl, p2h, p2l, qh, ql,
    hsem, wsem, psem, msem, rs_send, rs_recv, x_sent, x_got,
    sp, sr, sleft, rz, rp,
):
    K, N = hist_ref.shape
    S = w1_ref.shape[0]
    R = S // H
    Rc = R // C
    Nh = N // H
    nK = K // N
    Z = T // 2
    h = lax.axis_index("hist")
    t = lax.axis_index("tcol")
    p = t // 2
    core = t % 2
    other = 1 - core
    tile = 32

    def split(source, high, low, rows, function=lambda v: v):
        @pl.loop(0, rows // tile)
        def _(i):
            at = pl.ds(pl.multiple_of(i * tile, tile), tile)
            a, b = halves(function(source[at, :]))
            high[at, :] = a
            low[at, :] = b

    def hist_copy(kb):
        return pltpu.make_async_copy(hist_ref.at[pl.ds(kb * N, N), :], hbuf.at[kb], hsem.at[kb])

    def w_copy(w, c, j):
        ref = (w1_ref, w2_ref)[w]
        return pltpu.make_async_copy(
            ref.at[pl.ds(j * R + c * Rc, Rc), :], wbuf.at[w, c, j], wsem.at[w, c, j]
        )

    def p_copy(b):
        return pltpu.make_async_copy(
            prop_ref.at[pl.ds(b * N, N), :], hbuf.at[b % nK], psem.at[b]
        )

    own_rows = pl.ds(pl.multiple_of(h * R, R), R)
    small = (
        pltpu.make_async_copy(e1_ref.at[own_rows, :], e1, msem.at[0]),
        pltpu.make_async_copy(inv1_ref, mat.at[0], msem.at[1]),
        pltpu.make_async_copy(link_ref, mat.at[1], msem.at[2]),
        pltpu.make_async_copy(inv2_ref, mat.at[2], msem.at[3]),
        pltpu.make_async_copy(e2_ref.at[own_rows, :], e2, msem.at[4]),
    )

    for kb in range(nK):
        hist_copy(kb).start()
    for c in range(C):
        for j in range(H):
            w_copy(0, c, j).start()
    small[0].start()

    barrier = pltpu.get_barrier_semaphore()

    def greet(device):
        pl.semaphore_signal(barrier, inc=1, device_id=device, device_id_type=MESH)

    for d in range(1, H):
        greet({"hist": lax.rem(h + d, H)})
    greet({"tcol": p * 2 + other})

    greet({"tcol": lax.rem(p + 1, Z) * 2 + core})
    greet({"tcol": lax.rem(p + Z - 1, Z) * 2 + core})

    for kb in range(nK):
        hist_copy(kb).wait()
        split(hbuf.at[kb], sh.at[kb], sl.at[kb], N, cubic_power)

    for c in range(C):
        for j in range(H):
            w_copy(1, c, j).start()
    for copy in small[1:]:
        copy.start()
    for b in range(nK):
        p_copy(b).start()

    def history_sum(w, c):
        for j in range(H):
            w_copy(w, c, j).wait()
            split(wbuf.at[w, c, j], wh.at[j], wl.at[j], Rc)

        for kb in range(nK):
            cols = pl.ds(kb * N, N)
            a = wh[:, :, cols].reshape(H * Rc, N)
            b = wl[:, :, cols].reshape(H * Rc, N)
            value = mm(a, sh[kb]) + mm(b, sh[kb]) + mm(a, sl[kb])
            value = value.reshape(H, Rc, N)
            if kb == 0:
                part[w, c] = value
            else:
                part[w, c] += value

    def rs_copy(c, d):
        dst = lax.rem(h + d, H)
        return pltpu.make_async_remote_copy(
            src_ref=part.at[0, c, dst], dst_ref=rs.at[c, d - 1],
            send_sem=rs_send.at[c, d - 1], recv_sem=rs_recv.at[c, d - 1],
            device_id={"hist": dst}, device_id_type=MESH,
        )

    def gathered(c):
        total = part[0, c, h]
        for d in range(1, H):
            rs_copy(c, d).wait_recv()
            total += rs[c, d - 1]
        return total

    def exchange(kind, d, source, target):
        dst = lax.rem(h + d, H)
        return pltpu.make_async_remote_copy(
            src_ref=source(dst), dst_ref=target(h, d),
            send_sem=x_sent.at[kind, d - 1], recv_sem=x_got.at[kind, d - 1],
            device_id={"hist": dst}, device_id_type=MESH,
        )

    def arrived(kind, d, target):
        src = lax.rem(h + H - d, H)
        ref = target(src, d)
        pltpu.make_async_remote_copy(
            src_ref=ref, dst_ref=ref,
            send_sem=x_sent.at[kind, d - 1], recv_sem=x_got.at[kind, d - 1],
            device_id={"hist": src}, device_id_type=MESH,
        ).wait_recv()

    plans = {}
    for c in range(C):
        plans[c] = (
            lambda dst, c=c: nsend.at[c, dst], lambda src, d, c=c: nrecv.at[c, d - 1])
        plans[C + c] = (
            lambda dst, c=c: rsend.at[c, dst], lambda src, d, c=c: rf.at[c, src])
        plans[2 * C + c] = (
            lambda dst, c=c: ysend.at[c, dst], lambda src, d, c=c: yrecv.at[c, src])
    plans[3 * C] = (lambda dst: s1.at[dst], lambda src, d: orecv.at[src])
    plans[3 * C + 1] = (lambda dst: bsend.at[dst], lambda src, d: brecv.at[src])

    def x_start(kind):
        for d in range(1, H):
            exchange(kind, d, *plans[kind]).start()

    def x_wait(kind):
        for d in range(1, H):
            arrived(kind, d, plans[kind][1])

    def z_copy(g, st, c, q, where):
        block = g.at[c, 2 * q + core]
        send, recv, target = {
            "partner": (sp, rp, p * 2 + other),
            "right": (sr, rz, t + 2),
            "left": (sleft, rz, t - 2),
        }[where]
        return pltpu.make_async_remote_copy(
            src_ref=block, dst_ref=block,
            send_sem=send.at[st, c, q], recv_sem=recv.at[st, c, q],
            device_id={"tcol": target}, device_id_type=MESH,
        )

    def z_partner_wait(g, st, c, q):
        block = g.at[c, 2 * q + other]
        pltpu.make_async_remote_copy(
            src_ref=block, dst_ref=block,
            send_sem=sp.at[st, c, q], recv_sem=rp.at[st, c, q],
            device_id={"tcol": p * 2 + other}, device_id_type=MESH,
        ).wait_recv()

    def z_own(g, st, c):
        @pl.when(p + 1 < Z)
        def _():
            z_copy(g, st, c, p, "right").start()

        @pl.when(p > 0)
        def _():
            z_copy(g, st, c, p, "left").start()

        z_copy(g, st, c, p, "partner").start()

    def z_step(g, st, c, s, use):
        @pl.when(p >= s)
        def _():
            q = p - s
            z_copy(g, st, c, q, "right").wait_recv()

            @pl.when(p + 1 < Z)
            def _():
                z_copy(g, st, c, q, "right").start()

            z_copy(g, st, c, q, "partner").start()

        @pl.when(p + s < Z)
        def _():
            q = p + s
            z_copy(g, st, c, q, "left").wait_recv()

            @pl.when(p > 0)
            def _():
                z_copy(g, st, c, q, "left").start()

            z_copy(g, st, c, q, "partner").start()

        @pl.when(p >= s)
        def _():
            use(c, 2 * (p - s) + core)

        @pl.when(p + s < Z)
        def _():
            use(c, 2 * (p + s) + core)

        @pl.when(p >= s)
        def _():
            z_partner_wait(g, st, c, p - s)
            use(c, 2 * (p - s) + other)

        @pl.when(p + s < Z)
        def _():
            z_partner_wait(g, st, c, p + s)
            use(c, 2 * (p + s) + other)

    def z_finish(g, st, c):
        z_copy(g, st, c, p, "partner").wait_send()

        @pl.when(p + 1 < Z)
        def _():
            z_copy(g, st, c, p, "right").wait_send()

        @pl.when(p > 0)
        def _():
            z_copy(g, st, c, p, "left").wait_send()

        for s in range(1, Z):
            @pl.when(p >= s)
            def _():
                z_copy(g, st, c, p - s, "partner").wait_send()

                @pl.when(p + 1 < Z)
                def _():
                    z_copy(g, st, c, p - s, "right").wait_send()

            @pl.when(p + s < Z)
            def _():
                z_copy(g, st, c, p + s, "partner").wait_send()

                @pl.when(p > 0)
                def _():
                    z_copy(g, st, c, p + s, "left").wait_send()

    def use_one(c, b):
        acc1[c] += product(g1[c, b], ph[b], plo[b])

    def use_two(c, b):
        acc2[c] += product(g2[c, b], ph[b], plo[b])

    history_sum(0, 0)
    pl.semaphore_wait(barrier, H + 2)

    for d in range(1, H):
        rs_copy(0, d).start()
    for c in range(1, C):
        history_sum(0, c)
        for d in range(1, H):
            rs_copy(c, d).start()

    small[0].wait()

    def begin_one(c):
        value = gathered(c) + e1[pl.ds(c * Rc, Rc), :]
        pred[c] = value
        g1[c, t] = cubic_power(value)
        z_own(g1, 0, c)

    for b in range(T):
        p_copy(b).wait()
        split(hbuf.at[b % nK], ph.at[b], plo.at[b], N)
        if b + nK < T:
            p_copy(b + nK).start()

    small[4].wait()

    def near_sums(c):
        history_sum(1, c)
        part[1, c, h] += e2[pl.ds(c * Rc, Rc), :]
        for j in range(H):
            nsend[c, j] = part[1, c, :, :, j * Nh:(j + 1) * Nh]
        x_start(c)

    def local_one(c):
        acc1[c] = product(g1[c, t], ph[t], plo[t])
        z_partner_wait(g1, 0, c, p)
        use_one(c, 2 * p + other)

    begin_one(0)
    near_sums(0)
    for c in range(1, C):
        begin_one(c)
    for c in range(C):
        local_one(c)
        z_step(g1, 0, c, 1, use_one)
    for c in range(1, C):
        near_sums(c)

    for copy in small[1:4]:
        copy.wait()
    split(mat.at[0], ih, il, S)
    split(mat.at[1], kh, kl, S)
    split(mat.at[2], vh, vl, S)

    def send_right(c):
        value = pred[c] + step_size * acc1[c]
        for j in range(H):
            rsend[c, j] = value[:, j * Nh:(j + 1) * Nh]
        x_start(C + c)
        rf[c, h] = rsend[c, h]

    def sum_near():
        for c in range(C):
            x_wait(c)
            total = nsend[c, h]
            for d in range(1, H):
                total += nrecv[c, d - 1]
            near[:, c] = total

    for s in range(2, Z):
        for c in range(C):
            z_step(g1, 0, c, s, use_one)
            if s == Z - 1:
                send_right(c)
    if Z == 2:
        for c in range(C):
            send_right(c)
    sum_near()

    for c in range(C):
        x_wait(C + c)

        @pl.loop(0, H)
        def _(j):
            a, b = halves(rf[c, j])
            xh[j, c] = a
            xl[j, c] = b

    def apply(high, low, j, a, b):
        rows = pl.ds(pl.multiple_of(j * R, R), R)
        left, rest = high[rows, :], low[rows, :]
        return mm(left, a) + mm(rest, a) + mm(left, b)

    a, b = xh[...].reshape(S, Nh), xl[...].reshape(S, Nh)

    @pl.loop(0, H)
    def _(j):
        value = apply(ih, il, j, a, b)
        s1[j] = value
        p2h[j], p2l[j] = halves(cubic_power(value))

    a, b = p2h[...].reshape(S, Nh), p2l[...].reshape(S, Nh)

    @pl.loop(0, H)
    def _(j):
        value = apply(kh, kl, j, a, b) + near[j].reshape(R, Nh)
        s2[j] = value
        qh[j], ql[j] = halves(step_size * cubic_power(value))

    a, b = qh[...].reshape(S, Nh), ql[...].reshape(S, Nh)

    @pl.loop(0, H)
    def _(j):
        value = apply(vh, vl, j, a, b)
        for c in range(C):
            ysend[c, j] = value[c * Rc:(c + 1) * Rc, :]

    for c in range(C):
        x_start(2 * C + c)
        yrecv[c, h] = ysend[c, h]
    x_start(3 * C)
    orecv[h] = s1[h]

    @pl.loop(0, H)
    def _(j):
        p2h[j], p2l[j] = halves(s2[j])

    a, b = p2h[...].reshape(S, Nh), p2l[...].reshape(S, Nh)

    @pl.loop(0, H)
    def _(j):
        bsend[j] = apply(vh, vl, j, a, b)

    def begin_two(c):
        x_wait(2 * C + c)
        g2[c, t] = jnp.concatenate([yrecv[c, j] for j in range(H)], axis=1)
        z_own(g2, 1, c)

    def local_two(c):
        acc2[c] = product(g2[c, t], ph[t], plo[t])
        z_partner_wait(g2, 1, c, p)
        use_two(c, 2 * p + other)

    for c in range(C):
        begin_two(c)
    x_start(3 * C + 1)
    brecv[h] = bsend[h]
    for c in range(C):
        local_two(c)
        z_step(g2, 1, c, 1, use_two)
    x_wait(3 * C)
    for j in range(H):
        o1_ref[:, j * Nh:(j + 1) * Nh] = orecv[j]
    for s in range(2, Z):
        for c in range(C):
            z_step(g2, 1, c, s, use_two)
    x_wait(3 * C + 1)
    for c in range(C):
        rows = pl.ds(c * Rc, Rc)
        o2_ref[rows, :] = acc2[c] + jnp.concatenate([brecv[j, rows, :] for j in range(H)], axis=1)

    for c in range(C):
        for d in range(1, H):
            rs_copy(c, d).wait_send()
        z_finish(g1, 0, c)
        z_finish(g2, 1, c)
    for kind in range(3 * C + 2):
        for d in range(1, H):
            exchange(kind, d, *plans[kind]).wait_send()


def shards(*operands):
    history, w1 = operands[:2]
    K, N = history.shape
    S = w1.shape[0]
    H, T, C = lax.axis_size("hist"), lax.axis_size("tcol"), 2
    R = S // H
    Rc, Nh, nK, Z = R // C, N // H, K // N, T // 2
    V, D = pltpu.VMEM, pltpu.SemaphoreType.DMA
    return pl.pallas_call(
        functools.partial(kernel, H, T, C),
        out_shape=[jax.ShapeDtypeStruct((R, N), f32)] * 2,
        in_specs=[pl.BlockSpec(memory_space=pl.ANY)] * 9,
        out_specs=[pl.BlockSpec(memory_space=pltpu.VMEM)] * 2,
        scratch_shapes=[
            V((nK, N, N), f32), V((2, C, H, Rc, K), f32),
            V((H, Rc, K), bf16), V((H, Rc, K), bf16),
            V((nK, N, N), bf16), V((nK, N, N), bf16),
            V((T, N, N), bf16), V((T, N, N), bf16),
            V((3, S, S), f32),
            *[V((S, S), bf16)] * 6,
            V((R, N), f32), V((R, N), f32),
            V((2, C, H, Rc, N), f32), V((C, H - 1, Rc, N), f32),
            V((C, Rc, N), f32), V((C, Rc, N), f32), V((C, Rc, N), f32),
            V((C, T, Rc, N), f32), V((C, T, Rc, N), f32),
            V((C, H, H, Rc, Nh), f32), V((C, H - 1, H, Rc, Nh), f32), V((H, C, Rc, Nh), f32),
            V((C, H, Rc, Nh), f32), V((C, H, Rc, Nh), f32),
            V((H, R, Nh), f32), V((H, R, Nh), f32), V((H, R, Nh), f32),
            V((C, H, Rc, Nh), f32), V((C, H, Rc, Nh), f32),
            V((H, R, Nh), f32), V((H, R, Nh), f32),
            V((H, C, Rc, Nh), bf16), V((H, C, Rc, Nh), bf16),
            *[V((H, R, Nh), bf16)] * 4,
            D((nK,)), D((2, C, H)), D((T,)), D((5,)),
            D((C, H - 1)), D((C, H - 1)), D((3 * C + 2, H - 1)), D((3 * C + 2, H - 1)),
            D((2, C, Z)), D((2, C, Z)), D((2, C, Z)), D((2, C, Z)), D((2, C, Z)),
        ],
        compiler_params=pltpu.CompilerParams(
            collective_id=0, has_side_effects=True, vmem_limit_bytes=64 * 1024 * 1024 - 65536
        ),
    )(*operands)


def solution(mesh):
    return jax.shard_map(
        shards,
        mesh=mesh,
        in_specs=(
            P("hist", "tcol"),
            P(None, "hist"),
            P(None, "hist"),
            P(),
            P(None, "tcol"),
            P(),
            P(),
            P(None, "tcol"),
            P(None, "tcol"),
        ),
        out_specs=(P("hist", "tcol"), P("hist", "tcol")),
        check_vma=False,
    )
```
